256 devices in a mesh: reg: 64 (over z, y, core), ep: 4 (over x).
Axes of the slice: x: 4, y: 4, z: 8, core: 2. Of those that a mesh axis runs over, the one named last changes fastest.
Arguments:
- log_prices: bfloat16 [256, 64, 256], P('reg', 'ep'), may hold values from -3 to 3
- log_wages: float32 [256, 64], P('reg', 'ep'), may hold values from -12 to 1
- labor_share: float32 [256, 256], P('reg'), may hold values from 0.3 to 0.7
- io_coeffs: bfloat16 [256, 256, 256], P('reg'), may hold values from -0.375 to 0.375
- pair_blocks: bfloat16 [256, 32, 256, 256], P('reg'), may hold values from -0.0201 to 0.801
- log_tau: float32 [256, 32, 256], P('reg'), may hold values from 0.05 to 2
- elasticity: float32 [256], replicated, may hold values from 2 to 40
- partners: int32 [256, 32], replicated, may hold values from 0 to 255, as said below
- list_lengths: int32 [256], replicated, may hold values from 1 to 32, as said below
- price_cotangent: float32 [256, 64, 256], P('reg', 'ep'), may hold values from -6 to 6
Outputs:
- new_prices: bfloat16 [256, 64, 256], P('reg', 'ep')
- price_grad: float32 [256, 64, 256], P('reg', 'ep')
- wage_grad: float32 [256, 64], P('reg', 'ep')
- tau_grad: float32 [256, 32, 256], P('reg')
The draws below stay inside these ranges and needn't reach their ends.
Inputs may be any that keep to these rules, and one draw needn't show every extreme that they name: `partners`: each list names distinct regions. Over their live entries, the 4 importers of an aligned block name at most 2 regions of any one aligned block of 4 regions, and this is reached in every draw. `list_lengths`: in some aligned block of 4 regions every list has 32 live entries.
All inputs are finite; a program needn't handle non-finite values.
Results may differ from the reference program's by a relative error of at most 0.0064.
Values may be sent and summed in bfloat16 or wider, within the bound.
A program may use at most 64 MiB of HBM per device.

```python
import math
import jax
import jax.numpy as jnp
from jax import lax

J = 256
REG_DEV = 4
LMAX = 32
REGIONS = 256
EPISODES = 64


def draw_log_wages(key, part):
    first_key = jax.random.fold_in(jax.random.fold_in(key, 7), 0)
    return jnp.clip(0.5 * jax.random.normal(first_key, (REGIONS, EPISODES), jnp.float32), -12.0, 1.0)


def draw_pair_blocks(key, part):
    first_key, second_key = jax.random.split(jax.random.fold_in(key, 13), 2)
    shape_full = (REGIONS, LMAX, J, J)
    diagonal = jax.random.uniform(first_key, shape_full, jnp.float32, 0.4, 0.8)
    spread = jax.random.uniform(second_key, shape_full, jnp.float32, -0.02, 0.02)
    rows_index = jax.lax.broadcasted_iota(jnp.int32, shape_full, 2)
    cols_index = jax.lax.broadcasted_iota(jnp.int32, shape_full, 3)
    return jnp.where(rows_index == cols_index, diagonal, spread).astype(jnp.bfloat16)


def draw_partners(key, part):
    blocks = REGIONS // REG_DEV
    first_key, second_key, third_key = jax.random.split(jax.random.fold_in(key, 11), 3)
    ordering = jax.random.randint(first_key, (REGIONS, LMAX), 0, 1 << 20) * LMAX + jnp.arange(LMAX, dtype=jnp.int32)[None, :]
    shuffled = jnp.argsort(ordering, axis=1, stable=True).astype(jnp.int32)
    rotation = jax.random.randint(second_key, (blocks,), 0, blocks)
    inner_shift = jax.random.randint(third_key, (blocks,), 0, REG_DEV)
    region_ids = jnp.arange(REGIONS, dtype=jnp.int32)
    block_ids = region_ids // REG_DEV
    global_slot = shuffled + (region_ids % REG_DEV * LMAX)[:, None]
    source_block = (global_slot + rotation[block_ids][:, None]) % blocks
    inner_index = (global_slot // blocks + inner_shift[block_ids][:, None]) % REG_DEV
    return (source_block * REG_DEV + inner_index).astype(jnp.int32)


def draw_list_lengths(key, part):
    blocks = REGIONS // REG_DEV
    first_key, second_key, third_key = jax.random.split(jax.random.fold_in(key, 23), 3)
    shorter = jax.random.randint(first_key, (REGIONS,), max(LMAX * 3 // 8, 1), LMAX + 1)
    longer = jax.random.randint(second_key, (REGIONS,), 0, 8) == 0
    full_block = jax.random.randint(third_key, (), 0, blocks)
    block_ids = jnp.arange(REGIONS, dtype=jnp.int32) // REG_DEV
    return jnp.where(longer | (block_ids == full_block), LMAX, shorter).astype(jnp.int32)


def level_of(stream_key, dims, shards, smallest, largest):
    gain = 1.0
    for axis_at, shards_of in shards:
        heights = jax.random.uniform(jax.random.fold_in(jax.random.fold_in(stream_key, 6), axis_at), (shards_of,), jnp.float32, smallest / len(shards), largest / len(shards))
        gain = gain * jnp.repeat(jnp.exp(heights), dims[axis_at] // shards_of).reshape((-1,) + (1,) * (len(dims) - 1 - axis_at))
    return gain


def bell_draw(rng, shape, deviation, reach, cuts=(), kind=jnp.bfloat16):
    result = jax.random.normal(rng, shape, jnp.float32) * deviation
    if len(cuts) > 0:
        result = level_of(rng, shape, cuts, -0.22, 0.18) * result
    return jnp.clip(result, min=-reach, max=reach).astype(kind)


def setup_inputs(seed: int = 0) -> dict:
    keys = jax.random.split(jax.random.key(seed), 11)
    log_prices = bell_draw(keys[0], (REGIONS, EPISODES, J), 0.5, 3.0, ((0, 64), (1, 4)))
    log_wages = draw_log_wages(jax.random.fold_in(keys[10], 71), 0)
    labor_share = jnp.clip(0.3 + 0.39999998 * jax.random.uniform(keys[2], (REGIONS, J), jnp.float32) ** level_of(keys[2], (REGIONS, J), ((0, 64),), -0.2, 0.2), 0.3, 0.7)
    io_coeffs = bell_draw(keys[3], (REGIONS, J, J), J ** -0.5, 0.375, ((0, 64),))
    pair_blocks = draw_pair_blocks(jax.random.fold_in(keys[10], 71), 0)
    log_tau = jnp.clip(jnp.exp(math.log(2.0) - 3.6888794 * jax.random.uniform(keys[5], (REGIONS, LMAX, J), jnp.float32) ** level_of(keys[5], (REGIONS, LMAX, J), ((0, 64),), -0.2, 0.2)), 0.05, 2.0)
    elasticity = jnp.clip(jnp.exp(jax.random.uniform(keys[6], (J,), jnp.float32, math.log(2.0), math.log(40.0))), 2.0, 40.0)
    partners = draw_partners(jax.random.fold_in(keys[10], 71), 0)
    list_lengths = draw_list_lengths(jax.random.fold_in(keys[10], 71), 0)
    price_cotangent = bell_draw(keys[9], (REGIONS, EPISODES, J), 1.0, 6.0, ((0, 64), (1, 4)), jnp.float32)
    return {"log_prices": log_prices, "log_wages": log_wages, "labor_share": labor_share, "io_coeffs": io_coeffs, "pair_blocks": pair_blocks, "log_tau": log_tau, "elasticity": elasticity, "partners": partners, "list_lengths": list_lengths, "price_cotangent": price_cotangent}


def reference(log_prices, log_wages, labor_share, io_coeffs, pair_blocks, log_tau, elasticity, partners, list_lengths, price_cotangent):
    combined = labor_share[:, None, :] * log_wages[:, :, None] + jnp.einsum("iek,ikj->iej", log_prices.astype(jnp.float32), io_coeffs.astype(jnp.float32))
    unit_cost = lax.optimization_barrier(combined.astype(jnp.bfloat16))
    slot_index = jnp.arange(LMAX, dtype=jnp.int32)

    def importer(pushed_total, inputs):
        partner_row, length, block, tau_row, cotangent = inputs
        exporter_rows = unit_cost[partner_row].astype(jnp.float32)
        block_wide = block.astype(jnp.float32)
        landed = tau_row[:, None, :] + jnp.einsum("sek,skj->sej", exporter_rows, block_wide)
        live = (slot_index < length)[:, None, None]
        scores = jnp.where(live, -elasticity * landed, -jnp.inf)
        top_score = jnp.max(scores, axis=0)
        weights = jnp.exp(scores - top_score)
        total = jnp.sum(weights, axis=0)
        new_price = -(top_score + jnp.log(total)) / elasticity
        adjoint = cotangent[None] * (weights / total)
        tau_grad = jnp.sum(adjoint, axis=1)
        rounded = lax.optimization_barrier(adjoint.astype(jnp.bfloat16)).astype(jnp.float32)
        pushed = lax.optimization_barrier(jnp.einsum("sej,skj->sek", rounded, block_wide).astype(jnp.bfloat16))
        pushed_wide = jnp.where(live, pushed.astype(jnp.float32), jnp.float32(0.0))
        return pushed_total.at[partner_row].add(pushed_wide), (new_price, tau_grad)

    initial = jnp.zeros((REGIONS, EPISODES, J), jnp.float32)
    cost_adjoint, outputs = lax.scan(importer, initial, (partners, list_lengths, pair_blocks, log_tau, price_cotangent))
    new_prices, tau_grad = outputs
    cost_rounded = lax.optimization_barrier(cost_adjoint.astype(jnp.bfloat16)).astype(jnp.float32)
    price_grad = jnp.einsum("iej,ikj->iek", cost_rounded, io_coeffs.astype(jnp.float32))
    wage_grad = jnp.sum(cost_adjoint * labor_share[:, None, :], axis=2)
    return new_prices.astype(jnp.bfloat16), price_grad, wage_grad, tau_grad
```

```python
import jax
import jax.numpy as jnp
from jax import lax
from jax.experimental import pallas as pl
from jax.experimental.pallas import tpu as pltpu
from jax.sharding import PartitionSpec as P

NZ, NY, NC = 8, 4, 2
OUT = (0, 1, 7, 2, 6, 3, 5, 4)
F32 = jnp.float32
BF16 = jnp.bfloat16
MESH = pl.DeviceIdType.MESH
VMEM = pl.BlockSpec(memory_space=pltpu.VMEM)
ANY = pl.BlockSpec(memory_space=pl.ANY)
DMA = pltpu.SemaphoreType.DMA


def place():
    me = lax.axis_index("reg")
    return me // (NY * NC), (me // NC) % NY, me % NC


def at(z, y, c):
    return {"reg": (z * NY + y) * NC + c}


def greet(z, y, c, across):
    barrier = pltpu.get_barrier_semaphore()
    peers = [at((z + d) % NZ, y, c) for d in range(1, NZ)]
    peers += [at(z, (y + 1) % NY, c), at(z, (y + NY - 1) % NY, c), at(z, y, 1 - c)]
    if across:
        here = lax.axis_index("ep")
        size = lax.axis_size("ep")
        peers += [{"ep": (here + d) % size} for d in range(1, size)]
    for peer in peers:
        pl.semaphore_signal(barrier, inc=1, device_id=peer, device_id_type=MESH)
    return barrier, len(peers)


def gather_kernel(
    prices, wages, share, io, rows,
    z_send, z_recv, y_send, y_recv, h_send, h_recv, c_send, c_recv,
):
    z, y, c = place()
    right, left, across = (y + 1) % NY, (y + NY - 1) % NY, (y + 2) % NY
    barrier, count = greet(z, y, c, False)
    episodes = prices.shape[1]
    eye = lax.broadcasted_iota(jnp.int32, (episodes, episodes), 0) == lax.broadcasted_iota(
        jnp.int32, (episodes, episodes), 1
    )
    for i in range(prices.shape[0]):
        column = jnp.sum(
            jnp.where(eye, wages[i : i + 1, :], 0.0), axis=1, keepdims=True
        )
        cost = column * share[i : i + 1, :] + jnp.dot(
            prices[i], io[i], preferred_element_type=F32
        )
        rows[z, y, c, i] = cost.astype(BF16)
    pl.semaphore_wait(barrier, count)

    def copy(block, ssem, rsem, dev):
        return pltpu.make_async_remote_copy(
            src_ref=block, dst_ref=block, send_sem=ssem, recv_sem=rsem,
            device_id=dev, device_id_type=MESH,
        )

    sends = []

    def go(block, ssem, rsem, dev):
        one = copy(block, ssem, rsem, dev)
        one.start()
        sends.append(one)

    own = rows.at[z, y, c]
    go(own, y_send.at[0, 0], y_recv.at[0, 0], at(z, right, c))
    go(own, y_send.at[0, 1], y_recv.at[0, 1], at(z, left, c))
    for d in OUT[1:]:
        go(own, z_send.at[d], z_recv.at[d], at((z + d) % NZ, y, c))
    half = prices.shape[0] // 2
    for t in range(NZ + 2):
        if 0 < t < NZ:
            d = OUT[t]
            zz = (z + NZ - d) % NZ
            block = rows.at[zz, y, c]
            copy(block, z_send.at[d], z_recv.at[d], at(z, y, c)).wait_recv()
            go(block, y_send.at[t, 0], y_recv.at[t, 0], at(z, right, c))
            go(block, y_send.at[t, 1], y_recv.at[t, 1], at(z, left, c))
        if 0 < t < NZ + 1:
            k = t - 1
            zz = (z + NZ - OUT[k]) % NZ
            block = rows.at[zz, left, c]
            copy(block, y_send.at[k, 0], y_recv.at[k, 0], at(z, y, c)).wait_recv()
            go(block.at[:half], h_send.at[k, 0], h_recv.at[k, 0], at(z, right, c))
            block = rows.at[zz, right, c]
            copy(block, y_send.at[k, 1], y_recv.at[k, 1], at(z, y, c)).wait_recv()
            go(block.at[half:], h_send.at[k, 1], h_recv.at[k, 1], at(z, left, c))
        if t > 1:
            k = t - 2
            zz = (z + NZ - OUT[k]) % NZ
            block = rows.at[zz, across, c]
            copy(block.at[:half], h_send.at[k, 0], h_recv.at[k, 0], at(z, y, c)).wait_recv()
            copy(block.at[half:], h_send.at[k, 1], h_recv.at[k, 1], at(z, y, c)).wait_recv()
            go(rows.at[zz, :, c], c_send.at[k], c_recv.at[k], at(z, y, 1 - c))
    for k in range(NZ):
        zz = (z + NZ - OUT[k]) % NZ
        copy(rows.at[zz, :, 1 - c], c_send.at[k], c_recv.at[k], at(z, y, c)).wait_recv()
    for one in sends:
        one.wait_send()


def slots_kernel(
    rows, blocks, tau, elasticity, partners, lengths, cotangent,
    prices_out, tau_out, pushed_out,
    weights, held, who, how, adjoint, b_sem, w_sem,
):
    regions, slots = blocks.shape[0], blocks.shape[1]
    episodes, sectors = cotangent.shape[1], cotangent.shape[2]
    step = slots // held_chunks(slots)
    chunks = slots // step
    me = lax.axis_index("reg")
    base = (me // 2) * 8
    inner = (me % 2) * regions
    copies = [
        pltpu.make_async_copy(partners.at[pl.ds(pl.multiple_of(base, 8), 8)], who, w_sem.at[0]),
        pltpu.make_async_copy(lengths, how, w_sem.at[1]),
    ]
    for one in copies:
        one.start()
    for n in range(regions):
        for q in range(chunks):
            part = pl.ds(q * step, step)
            pltpu.make_async_copy(
                blocks.at[n, part], held.at[n, part], b_sem.at[n * chunks + q]
            ).start()
    pushed_out[...] = jnp.zeros_like(pushed_out)
    for one in copies:
        one.wait()
    slope = -elasticity[...]
    for n in range(regions):
        length = how[me * regions + n]
        top = jnp.full((episodes, sectors), -jnp.inf, F32)
        for q in range(chunks):
            part = pl.ds(q * step, step)
            pltpu.make_async_copy(
                blocks.at[n, part], held.at[n, part], b_sem.at[n * chunks + q]
            ).wait()

            for s in range(q * step, (q + 1) * step):
                landed = tau[n, s : s + 1, :] + jnp.dot(
                    rows[who[inner + n, s]], held[n, s], preferred_element_type=F32
                )
                score = jnp.where(s < length, slope * landed, -jnp.inf)
                weights[s] = score
                top = jnp.maximum(top, score)
        total = jnp.zeros((episodes, sectors), F32)
        for s in range(slots):
            one = jnp.exp(weights[s] - top)
            weights[s] = one
            total = total + one
        prices_out[n] = (-(top + jnp.log(total)) / elasticity[...]).astype(BF16)
        scale = cotangent[n] / total
        for s in range(slots):
            one = weights[s] * scale
            tau_out[n, s : s + 1, :] = jnp.sum(one, axis=0, keepdims=True)
            pushed = lax.dot_general(
                one.astype(BF16), held[n, s], (((1,), (1,)), ((), ())),
                preferred_element_type=F32,
            ).astype(BF16)
            row = who[inner + n, s]
            pushed_out[row] = (pushed_out[row].astype(F32) + pushed.astype(F32)).astype(BF16)


def held_chunks(slots):
    return 4


def scatter_kernel(
    pushed, tau, share, io,
    price_grad, wage_grad, tau_grad,
    from_core, far, near, mine, a_recv, b_recv, z_in, x_in,
    c_send, c_recv, a_send, a_rsem, b_send, b_rsem, z_send, z_rsem, x_send, x_rsem,
):
    z, y, c = place()
    right, left, across = (y + 1) % NY, (y + NY - 1) % NY, (y + 2) % NY
    here = lax.axis_index("ep")
    size = lax.axis_size("ep")
    barrier, count = greet(z, y, c, True)
    pl.semaphore_wait(barrier, count)
    half = pushed.shape[3] // 2
    sends = []

    def copy(src, dst, ssem, rsem, dev):
        return pltpu.make_async_remote_copy(
            src_ref=src, dst_ref=dst, send_sem=ssem, recv_sem=rsem,
            device_id=dev, device_id_type=MESH,
        )

    def go(*args):
        one = copy(*args)
        one.start()
        sends.append(one)
        return one

    order = OUT[::-1]
    arrivals = []
    for k in range(NZ):
        zz = (z + order[k]) % NZ
        arrivals.append(
            go(pushed.at[zz, :, 1 - c], from_core.at[k], c_send.at[k], c_recv.at[k], at(z, y, 1 - c))
        )
    tau_moves = [
        go(tau, x_in.at[here], x_send.at[d], x_rsem.at[d], {"ep": (here + d) % size})
        for d in range(1, size)
    ]
    x_in[here] = tau[...]

    def chip(k, yy, part):
        zz = (z + order[k]) % NZ
        return pushed[zz, yy, c, part].astype(F32) + from_core[k, yy, part].astype(F32)

    lo, hi, whole = pl.ds(0, half), pl.ds(half, half), pl.ds(0, 2 * half)
    a_moves, b_moves, z_moves = {}, {}, {}
    for t in range(NZ + 2):
        if t < NZ:
            k = t
            arrivals[k].wait_recv()
            far[k] = chip(k, across, whole).astype(BF16)
            a_moves[k] = (
                go(far.at[k, lo], a_recv.at[k, 0], a_send.at[k, 0], a_rsem.at[k, 0], at(z, right, c)),
                go(far.at[k, hi], a_recv.at[k, 1], a_send.at[k, 1], a_rsem.at[k, 1], at(z, left, c)),
            )
        if 0 < t < NZ + 1:
            k = t - 1
            a_moves[k][0].wait_recv()
            near[k, 0, lo] = (chip(k, right, lo) + a_recv[k, 0].astype(F32)).astype(BF16)
            near[k, 0, hi] = chip(k, right, hi).astype(BF16)
            a_moves[k][1].wait_recv()
            near[k, 1, lo] = chip(k, left, lo).astype(BF16)
            near[k, 1, hi] = (chip(k, left, hi) + a_recv[k, 1].astype(F32)).astype(BF16)
            b_moves[k] = (
                go(near.at[k, 0], b_recv.at[k, 0], b_send.at[k, 0], b_rsem.at[k, 0], at(z, right, c)),
                go(near.at[k, 1], b_recv.at[k, 1], b_send.at[k, 1], b_rsem.at[k, 1], at(z, left, c)),
            )
        if t > 1:
            k = t - 2
            for one in b_moves[k]:
                one.wait_recv()
            summed = (
                chip(k, y, whole) + b_recv[k, 0].astype(F32) + b_recv[k, 1].astype(F32)
            )
            if order[k]:
                mine[k] = summed.astype(BF16)
                z_moves[k] = go(
                    mine.at[k], z_in.at[k], z_send.at[k], z_rsem.at[k],
                    at((z + order[k]) % NZ, y, c),
                )
            else:
                final = summed
    for k in range(NZ - 1):
        z_moves[k].wait_recv()
        final = final + z_in[k].astype(F32)
    episodes = final.shape[1]
    eye = lax.broadcasted_iota(jnp.int32, (episodes, episodes), 0) == lax.broadcasted_iota(
        jnp.int32, (episodes, episodes), 1
    )
    for i in range(final.shape[0]):
        price_grad[i] = lax.dot_general(
            final[i].astype(BF16), io[i], (((1,), (1,)), ((), ())), preferred_element_type=F32
        )
        column = jnp.sum(final[i] * share[i : i + 1, :], axis=1, keepdims=True)
        wage_grad[i : i + 1, :] = jnp.sum(
            jnp.where(eye, column, 0.0), axis=0, keepdims=True
        )
    for one in tau_moves:
        one.wait_recv()
    tau_grad[...] = (x_in[0] + x_in[1]) + (x_in[2] + x_in[3])
    for one in sends:
        one.wait_send()


def shards(
    log_prices,
    log_wages,
    labor_share,
    io_coeffs,
    pair_blocks,
    log_tau,
    elasticity,
    partners,
    list_lengths,
    price_cotangent,
):
    own, episodes, sectors = log_prices.shape
    slots = pair_blocks.shape[1]
    block = (own, episodes, sectors)
    total = NZ * NY * NC * own
    rows = pl.pallas_call(
        gather_kernel,
        out_shape=jax.ShapeDtypeStruct((NZ, NY, NC) + block, BF16),
        in_specs=[VMEM] * 4,
        out_specs=VMEM,
        scratch_shapes=[
            DMA((NZ,)), DMA((NZ,)), DMA((NZ, 2)), DMA((NZ, 2)),
            DMA((NZ, 2)), DMA((NZ, 2)), DMA((NZ,)), DMA((NZ,)),
        ],
        compiler_params=pltpu.CompilerParams(collective_id=0, has_side_effects=True),
        name="gather_costs",
    )(log_prices, log_wages, labor_share, io_coeffs)

    chunks = held_chunks(slots)
    new_prices, tau_part, pushed = pl.pallas_call(
        slots_kernel,
        out_shape=(
            jax.ShapeDtypeStruct(block, BF16),
            jax.ShapeDtypeStruct((own, slots, sectors), F32),
            jax.ShapeDtypeStruct((total, episodes, sectors), BF16),
        ),
        in_specs=[VMEM, ANY, VMEM, VMEM, ANY, ANY, VMEM],
        out_specs=(VMEM, VMEM, VMEM),
        scratch_shapes=[
            pltpu.VMEM((slots, episodes, sectors), F32),
            pltpu.VMEM((own, slots, sectors, sectors), BF16),
            pltpu.SMEM((8, slots), jnp.int32),
            pltpu.SMEM((total,), jnp.int32),
            pltpu.VMEM((slots, episodes, sectors), BF16),
            DMA((own * chunks,)),
            DMA((2,)),
        ],
        compiler_params=pltpu.CompilerParams(vmem_limit_bytes=40 << 20),
        name="slots",
    )(
        rows.reshape(total, episodes, sectors),
        pair_blocks,
        log_tau,
        elasticity.reshape(1, sectors),
        partners,
        list_lengths,
        price_cotangent,
    )

    half = (own // 2, episodes, sectors)
    price_grad, wage_grad, tau_grad = pl.pallas_call(
        scatter_kernel,
        out_shape=(
            jax.ShapeDtypeStruct(block, F32),
            jax.ShapeDtypeStruct((own, episodes), F32),
            jax.ShapeDtypeStruct((own, slots, sectors), F32),
        ),
        in_specs=[VMEM] * 4,
        out_specs=(VMEM,) * 3,
        scratch_shapes=[
            pltpu.VMEM((NZ, NY) + block, BF16),
            pltpu.VMEM((NZ,) + block, BF16),
            pltpu.VMEM((NZ, 2) + block, BF16),
            pltpu.VMEM((NZ,) + block, BF16),
            pltpu.VMEM((NZ, 2) + half, BF16),
            pltpu.VMEM((NZ, 2) + block, BF16),
            pltpu.VMEM((NZ,) + block, BF16),
            pltpu.VMEM((4, own, slots, sectors), F32),
            DMA((NZ,)), DMA((NZ,)), DMA((NZ, 2)), DMA((NZ, 2)), DMA((NZ, 2)), DMA((NZ, 2)),
            DMA((NZ,)), DMA((NZ,)), DMA((4,)), DMA((4,)),
        ],
        compiler_params=pltpu.CompilerParams(collective_id=1, has_side_effects=True),
        name="scatter_costs",
    )(pushed.reshape((NZ, NY, NC) + block), tau_part, labor_share, io_coeffs)
    return (new_prices, price_grad, wage_grad, tau_grad)


def solution(mesh):
    return jax.shard_map(
        shards,
        mesh=mesh,
        in_specs=(
            P("reg", "ep", None),
            P("reg", "ep"),
            P("reg", None),
            P("reg", None, None),
            P("reg", None, None, None),
            P("reg", None, None),
            P(),
            P(),
            P(),
            P("reg", "ep", None),
        ),
        out_specs=(
            P("reg", "ep", None),
            P("reg", "ep", None),
            P("reg", "ep"),
            P("reg", None, None),
        ),
        check_vma=False,
    )
```

```python
import jax
import jax.numpy as jnp
from jax import lax
from jax.experimental import pallas as pl
from jax.experimental.pallas import tpu as pltpu
from jax.sharding import PartitionSpec as P

NZ, NY, NC = 8, 4, 2
NEAR_FIRST = (1, 7, 2, 6, 3, 5, 4)
FAR_FIRST = (4, 5, 3, 6, 2, 7, 1, 0)
CHUNKS = 4
F32 = jnp.float32
BF16 = jnp.bfloat16
I32 = jnp.int32
MESH = pl.DeviceIdType.MESH
VMEM = pl.BlockSpec(memory_space=pltpu.VMEM)
ANY = pl.BlockSpec(memory_space=pl.ANY)
DMA = pltpu.SemaphoreType.DMA


def at(z, y, c):
    return {"reg": (z * NY + y) * NC + c}


def iota(shape, axis):
    return lax.broadcasted_iota(I32, shape, axis)


def fused_kernel(
    prices_in, wages_in, share_in, io_in, blocks, tau_in, slope_in, partners_in, lengths_in, cot_in,
    prices_out, price_grad, wage_grad, tau_sum,
    prices, wages, share, io, tau, elasticity, partners, lengths, cot, held, in_sem, b_sem,
    table, lookup, t_sem,
    rows, weights, pushed, tau_part,
    outgo, own, from_core, far, near, mine, a_in, b_in, z_in, x_in, cost,
    gz_s, gz_r, gy_s, gy_r, gh_s, gh_r, gc_s, gc_r,
    c_s, c_r, a_s, a_r, b_s, b_r, z_s, z_r, x_s, x_r,
):
    me = lax.axis_index("reg")
    z, y, c = me // (NY * NC), (me // NC) % NY, me % NC
    here, size = lax.axis_index("ep"), lax.axis_size("ep")
    right, left, across = (y + 1) % NY, (y + NY - 1) % NY, (y + 2) % NY
    regions, slots = blocks.shape[0], blocks.shape[1]
    episodes, sectors = cot.shape[1], cot.shape[2]
    total = rows.shape[0]
    half = regions // 2
    group = NY * regions

    barrier = pltpu.get_barrier_semaphore()
    peers = [at((z + d) % NZ, y, c) for d in range(1, NZ)]
    peers += [at(z, right, c), at(z, left, c), at(z, y, 1 - c)]
    peers += [{"ep": (here + d) % size} for d in range(1, size)]
    for peer in peers:
        pl.semaphore_signal(barrier, inc=1, device_id=peer, device_id_type=MESH)

    loads = [
        pltpu.make_async_copy(src, dst, in_sem.at[i])
        for i, (src, dst) in enumerate(
            (
                (io_in, io), (prices_in, prices), (wages_in, wages), (share_in, share),
                (partners_in, partners), (lengths_in, lengths), (slope_in, elasticity),
                (tau_in, tau), (cot_in, cot),
            )
        )
    ]
    for one in loads:
        one.start()
    step = slots // CHUNKS

    def block_load(n, q):
        part = pl.ds(q * step, step)
        return pltpu.make_async_copy(
            blocks.at[n, part], held.at[n, part], b_sem.at[n * CHUNKS + q]
        )

    for n in range(regions):
        for q in range(CHUNKS):
            block_load(n, q).start()

    sends = []

    def copy(src, dst, ssem, rsem, dev):
        return pltpu.make_async_remote_copy(
            src_ref=src, dst_ref=dst, send_sem=ssem, recv_sem=rsem,
            device_id=dev, device_id_type=MESH,
        )

    def go(*args):
        one = copy(*args)
        one.start()
        sends.append(one)
        return one

    def first(zz, cc, yy):
        return ((zz * NC + cc) * NY + yy) * regions

    for one in loads[:4]:
        one.wait()
    eye = iota((episodes, episodes), 0) == iota((episodes, episodes), 1)
    for i in range(regions):
        column = jnp.sum(jnp.where(eye, wages[i : i + 1, :], 0.0), axis=1, keepdims=True)
        unit = column * share[i : i + 1, :] + jnp.dot(
            prices[i], io[i], preferred_element_type=F32
        )
        rows[first(z, c, y) + i] = unit.astype(BF16)
    pl.semaphore_wait(barrier, len(peers))

    def block(zz, yy, off=0, count=regions):
        return rows.at[pl.ds(first(zz, c, yy) + off, count)]

    def shared(zz, cc):
        return rows.at[pl.ds(first(zz, cc, 0), group)]

    def push(ref, ssem, rsem, dev):
        go(ref, ref, ssem, rsem, dev)

    def land(ref, ssem, rsem):
        copy(ref, ref, ssem, rsem, at(z, y, c)).wait_recv()

    def both_ways(k, ref):
        push(ref, gy_s.at[k, 0], gy_r.at[k, 0], at(z, right, c))
        push(ref, gy_s.at[k, 1], gy_r.at[k, 1], at(z, left, c))

    mine_rows = block(z, y)
    for d in NEAR_FIRST[:2]:
        push(mine_rows, gz_s.at[d], gz_r.at[d], at((z + d) % NZ, y, c))
    both_ways(0, mine_rows)
    for d in NEAR_FIRST[2:]:
        push(mine_rows, gz_s.at[d], gz_r.at[d], at((z + d) % NZ, y, c))

    for one in loads[4:6]:
        one.wait()
    lanes = iota((slots, total), 1)
    rank = iota((slots, total), 0)
    lane_eye = rank == lanes
    for n in range(regions):
        pick = lanes == me * regions + n
        named = jnp.sum(jnp.where(pick, partners[...], 0), axis=1, keepdims=True)
        length = jnp.sum(jnp.where(pick[:1], lengths[...], 0), axis=1, keepdims=True)
        zz, yy, cc = named // (NY * NC * regions), (named // (NC * regions)) % NY, (named // regions) % NC
        named = first(zz, cc, yy) + named % regions
        live = rank < length
        where = jnp.min(
            jnp.where((named == lanes) & live, rank + n * slots, regions * slots),
            axis=0, keepdims=True,
        )
        table[n : n + 1, :] = where
        whom = jnp.sum(jnp.where(lane_eye, named, 0), axis=0, keepdims=True)
        table[regions + n : regions + n + 1, :] = jnp.where(lanes[:1] == slots, length, whom)
    pushed[regions * slots] = jnp.zeros((episodes, sectors), BF16)

    for d in NEAR_FIRST:
        ref = block((z + NZ - d) % NZ, y)
        land(ref, gz_s.at[d], gz_r.at[d])
        both_ways(d, ref)
    to_lookup = pltpu.make_async_copy(table, lookup, t_sem.at[0])
    to_lookup.start()
    for k in (0,) + NEAR_FIRST:
        zz = (z + NZ - k) % NZ
        land(block(zz, left), gy_s.at[k, 0], gy_r.at[k, 0])
        push(block(zz, left, 0, half), gh_s.at[k, 0], gh_r.at[k, 0], at(z, right, c))
        land(block(zz, right), gy_s.at[k, 1], gy_r.at[k, 1])
        push(block(zz, right, half, half), gh_s.at[k, 1], gh_r.at[k, 1], at(z, left, c))
    for k in (0,) + NEAR_FIRST:
        zz = (z + NZ - k) % NZ
        land(block(zz, across, 0, half), gh_s.at[k, 0], gh_r.at[k, 0])
        land(block(zz, across, half, half), gh_s.at[k, 1], gh_r.at[k, 1])
        push(shared(zz, c), gc_s.at[k], gc_r.at[k], at(z, y, 1 - c))
    to_lookup.wait()
    for one in loads[6:]:
        one.wait()
    for k in (0,) + NEAR_FIRST:
        land(shared((z + NZ - k) % NZ, 1 - c), gc_s.at[k], gc_r.at[k])

    def importer(n, carry):
        slope = -elasticity[...]
        length = lookup[regions + n, slots]
        top = jnp.full((episodes, sectors), -jnp.inf, F32)
        for q in range(CHUNKS):
            block_load(n, q).wait()
            for s in range(q * step, (q + 1) * step):
                landed = tau[n, s : s + 1, :] + jnp.dot(
                    rows[lookup[regions + n, s]], held[n, s], preferred_element_type=F32
                )
                score = jnp.where(s < length, slope * landed, -jnp.inf)
                weights[s] = score
                top = jnp.maximum(top, score)
        summed = jnp.zeros((episodes, sectors), F32)
        for s in range(slots):
            one = jnp.exp(weights[s] - top)
            weights[s] = one
            summed = summed + one
        prices_out[n] = (-(top + jnp.log(summed)) / elasticity[...]).astype(BF16)
        scale = cot[n] / summed
        for s in range(slots):
            one = weights[s] * scale
            tau_part[n, s : s + 1, :] = jnp.sum(one, axis=0, keepdims=True)
            pushed[n * slots + s] = lax.dot_general(
                one.astype(BF16), held[n, s], (((1,), (1,)), ((), ())),
                preferred_element_type=F32,
            ).astype(BF16)
        return carry

    lax.fori_loop(0, regions, importer, 0)

    def fill(dst, k, cc):
        base = first((z + FAR_FIRST[k]) % NZ, cc, 0)

        def some(r, carry):
            for i in range(regions):
                at_row = r * regions + i
                value = pushed[lookup[0, base + at_row]].astype(F32)
                for n in range(1, regions):
                    value = value + pushed[lookup[n, base + at_row]].astype(F32)
                dst[k, at_row] = value.astype(BF16)
            return carry

        lax.fori_loop(0, NY, some, 0)

    core_moves = []
    for k in range(NZ):
        fill(outgo, k, 1 - c)
        core_moves.append(
            go(outgo.at[k], from_core.at[k], c_s.at[k], c_r.at[k], at(z, y, 1 - c))
        )
    tau_moves = [
        go(tau_part, x_in.at[here], x_s.at[d], x_r.at[d], {"ep": (here + d) % size})
        for d in range(1, size)
    ]
    x_in[here] = tau_part[...]
    for k in range(NZ):
        fill(own, k, c)

    def chip(k, yy, off, count):
        part = pl.ds(yy * regions + off, count)
        return own[k, part].astype(F32) + from_core[k, part].astype(F32)

    a_moves, b_moves, z_moves = [], [], []
    for k in range(NZ):
        core_moves[k].wait_recv()
        far[k] = chip(k, across, 0, regions).astype(BF16)
        a_moves.append((
            go(far.at[k, :half], a_in.at[k, 0], a_s.at[k, 0], a_r.at[k, 0], at(z, right, c)),
            go(far.at[k, half:], a_in.at[k, 1], a_s.at[k, 1], a_r.at[k, 1], at(z, left, c)),
        ))
    for k in range(NZ):
        a_moves[k][0].wait_recv()
        near[k, 0, :half] = (chip(k, right, 0, half) + a_in[k, 0].astype(F32)).astype(BF16)
        near[k, 0, half:] = chip(k, right, half, half).astype(BF16)
        a_moves[k][1].wait_recv()
        near[k, 1, :half] = chip(k, left, 0, half).astype(BF16)
        near[k, 1, half:] = (chip(k, left, half, half) + a_in[k, 1].astype(F32)).astype(BF16)
        b_moves.append((
            go(near.at[k, 0], b_in.at[k, 0], b_s.at[k, 0], b_r.at[k, 0], at(z, right, c)),
            go(near.at[k, 1], b_in.at[k, 1], b_s.at[k, 1], b_r.at[k, 1], at(z, left, c)),
        ))
    for k in range(NZ):
        for one in b_moves[k]:
            one.wait_recv()
        summed = chip(k, y, 0, regions) + b_in[k, 0].astype(F32) + b_in[k, 1].astype(F32)
        d = FAR_FIRST[k]
        if d:
            mine[k] = summed.astype(BF16)
            z_moves.append(
                go(mine.at[k], z_in.at[k], z_s.at[k], z_r.at[k], at((z + d) % NZ, y, c))
            )
        else:
            cost[...] = summed
    for one in tau_moves:
        one.wait_recv()
    tau_sum[...] = (x_in[0] + x_in[1]) + (x_in[2] + x_in[3])
    for k in range(NZ - 1):
        z_moves[k].wait_recv()
    final = cost[...]
    for k in range(NZ - 1):
        final = final + z_in[k].astype(F32)
    for i in range(regions):
        price_grad[i] = lax.dot_general(
            final[i].astype(BF16), io[i], (((1,), (1,)), ((), ())), preferred_element_type=F32
        )
        column = jnp.sum(final[i] * share[i : i + 1, :], axis=1, keepdims=True)
        wage_grad[i : i + 1, :] = jnp.sum(jnp.where(eye, column, 0.0), axis=0, keepdims=True)
    for one in sends:
        one.wait_send()


def finish_kernel(*refs):
    count = (len(refs) - 2) // 3
    source, result, held = refs[:count], refs[count : 2 * count], refs[2 * count : 3 * count]
    in_sem, out_sem = refs[-2:]
    ins = [pltpu.make_async_copy(source[i], held[i], in_sem.at[i]) for i in range(count)]
    outs = [pltpu.make_async_copy(held[i], result[i], out_sem.at[i]) for i in range(count)]
    for one in ins:
        one.start()
    for one, then in zip(ins, outs):
        one.wait()
        then.start()
    for one in outs:
        one.wait()


def shards(
    log_prices,
    log_wages,
    labor_share,
    io_coeffs,
    pair_blocks,
    log_tau,
    elasticity,
    partners,
    list_lengths,
    price_cotangent,
):
    own, episodes, sectors = log_prices.shape
    slots = pair_blocks.shape[1]
    block = (own, episodes, sectors)
    half = (own // 2, episodes, sectors)
    group = (NY * own, episodes, sectors)
    total = NZ * NY * NC * own
    tau_shape = (own, slots, sectors)
    vm = pltpu.VMEM
    outs = (
        jax.ShapeDtypeStruct(block, BF16),
        jax.ShapeDtypeStruct(block, F32),
        jax.ShapeDtypeStruct((own, episodes), F32),
        jax.ShapeDtypeStruct(tau_shape, F32),
    )
    results = pl.pallas_call(
        fused_kernel,
        out_shape=outs,
        in_specs=[ANY] * 10,
        out_specs=(VMEM,) * 4,
        scratch_shapes=[
            vm(block, BF16), vm((own, episodes), F32), vm((own, sectors), F32),
            vm((own, sectors, sectors), BF16), vm(tau_shape, F32), vm((1, sectors), F32),
            vm((slots, total), I32), vm((1, total), I32), vm(block, F32),
            vm((own, slots, sectors, sectors), BF16), DMA((9,)), DMA((own * CHUNKS,)),
            vm((2 * own, total), I32), pltpu.SMEM((2 * own, total), I32), DMA((1,)),
            vm((total, episodes, sectors), BF16), vm((slots, episodes, sectors), F32),
            vm((own * slots + 1, episodes, sectors), BF16), vm(tau_shape, F32),
            vm((NZ,) + group, BF16), vm((NZ,) + group, BF16), vm((NZ,) + group, BF16),
            vm((NZ,) + block, BF16), vm((NZ, 2) + block, BF16), vm((NZ,) + block, BF16),
            vm((NZ, 2) + half, BF16), vm((NZ, 2) + block, BF16), vm((NZ,) + block, BF16),
            vm((4,) + tau_shape, F32), vm(block, F32),
            DMA((NZ,)), DMA((NZ,)), DMA((NZ, 2)), DMA((NZ, 2)), DMA((NZ, 2)), DMA((NZ, 2)),
            DMA((NZ,)), DMA((NZ,)),
            DMA((NZ,)), DMA((NZ,)), DMA((NZ, 2)), DMA((NZ, 2)), DMA((NZ, 2)), DMA((NZ, 2)),
            DMA((NZ,)), DMA((NZ,)), DMA((4,)), DMA((4,)),
        ],
        compiler_params=pltpu.CompilerParams(
            collective_id=0, has_side_effects=True, vmem_limit_bytes=60 * 1024 * 1024
        ),
        name="iteration",
    )(
        log_prices, log_wages, labor_share, io_coeffs, pair_blocks, log_tau,
        elasticity.reshape(1, sectors), partners.T, list_lengths.reshape(1, total),
        price_cotangent,
    )
    return pl.pallas_call(
        finish_kernel,
        out_shape=outs,
        in_specs=[ANY] * 4,
        out_specs=(ANY,) * 4,
        scratch_shapes=[vm(one.shape, one.dtype) for one in outs] + [DMA((4,)), DMA((4,))],
        compiler_params=pltpu.CompilerParams(vmem_limit_bytes=60 * 1024 * 1024),
        name="finish",
    )(*results)


def solution(mesh):
    return jax.shard_map(
        shards,
        mesh=mesh,
        in_specs=(
            P("reg", "ep", None),
            P("reg", "ep"),
            P("reg", None),
            P("reg", None, None),
            P("reg", None, None, None),
            P("reg", None, None),
            P(),
            P(),
            P(),
            P("reg", "ep", None),
        ),
        out_specs=(
            P("reg", "ep", None),
            P("reg", "ep", None),
            P("reg", "ep"),
            P("reg", None, None),
        ),
        check_vma=False,
    )
```

```python
import jax
import jax.numpy as jnp
from jax import lax
from jax.experimental import pallas as pl
from jax.experimental.pallas import tpu as pltpu
from jax.sharding import PartitionSpec as P

NZ, NY, NC = 8, 4, 2
FAR = (2, 6, 3, 5, 4)
BESIDE = (1, 7)
ORDER = (4, 5, 3, 1, 7, 6, 2, 0)
CHUNKS = 4
F32 = jnp.float32
BF16 = jnp.bfloat16
I32 = jnp.int32
MESH = pl.DeviceIdType.MESH
VMEM = pl.BlockSpec(memory_space=pltpu.VMEM)
ANY = pl.BlockSpec(memory_space=pl.ANY)
DMA = pltpu.SemaphoreType.DMA


def at(z, y, c):
    return {"reg": (z * NY + y) * NC + c}


def iota(shape, axis):
    return lax.broadcasted_iota(I32, shape, axis)


def fused_kernel(
    prices_in, wages_in, share_in, io_in, blocks, tau_in, slope_in, partners_in, lengths_in, cot_in,
    prices_out, price_grad, wage_grad, tau_sum,
    prices, wages, share, io, tau, elasticity, partners, lengths, cot, held, in_sem, b_sem,
    table, lookup, t_sem,
    rows, weights, pushed, tau_part,
    outgo, own, from_core, near, y_in, slab, v_in, mine, z_in, x_in,
    gz_s, gz_r, gy_s, gy_r, gv_s, gv_r, gc_s, gc_r,
    c_s, c_r, y_s, y_r, v_s, v_r, z_s, z_r, x_s, x_r,
):
    me = lax.axis_index("reg")
    z, y, c = me // (NY * NC), (me // NC) % NY, me % NC
    here, size = lax.axis_index("ep"), lax.axis_size("ep")
    right, left, across = (y + 1) % NY, (y + NY - 1) % NY, (y + 2) % NY
    regions, slots = blocks.shape[0], blocks.shape[1]
    episodes, sectors = cot.shape[1], cot.shape[2]
    total = rows.shape[0]
    group = NY * regions

    barrier = pltpu.get_barrier_semaphore()
    peers = [at((z + d) % NZ, y, c) for d in range(1, NZ)]
    peers += [at(z, right, c), at(z, left, c), at(z, across, c), at(z, y, 1 - c)]
    peers += [{"ep": (here + d) % size} for d in range(1, size)]
    for peer in peers:
        pl.semaphore_signal(barrier, inc=1, device_id=peer, device_id_type=MESH)

    loads = [
        pltpu.make_async_copy(src, dst, in_sem.at[i])
        for i, (src, dst) in enumerate(
            (
                (io_in, io), (prices_in, prices), (wages_in, wages), (share_in, share),
                (partners_in, partners), (lengths_in, lengths), (slope_in, elasticity),
                (tau_in, tau), (cot_in, cot),
            )
        )
    ]
    for one in loads:
        one.start()
    step = slots // CHUNKS

    def block_load(n, q):
        part = pl.ds(q * step, step)
        return pltpu.make_async_copy(
            blocks.at[n, part], held.at[n, part], b_sem.at[n * CHUNKS + q]
        )

    sends = []

    def copy(src, dst, ssem, rsem, dev):
        return pltpu.make_async_remote_copy(
            src_ref=src, dst_ref=dst, send_sem=ssem, recv_sem=rsem,
            device_id=dev, device_id_type=MESH,
        )

    def go(*args):
        one = copy(*args)
        one.start()
        sends.append(one)
        return one

    def first(zz, cc, yy):
        return ((zz * NC + cc) * NY + yy) * regions

    for one in loads[:4]:
        one.wait()
    eye = iota((episodes, episodes), 0) == iota((episodes, episodes), 1)
    for i in range(regions):
        column = jnp.sum(jnp.where(eye, wages[i : i + 1, :], 0.0), axis=1, keepdims=True)
        unit = column * share[i : i + 1, :] + jnp.dot(
            prices[i], io[i], preferred_element_type=F32
        )
        rows[first(z, c, y) + i] = unit.astype(BF16)
    pl.semaphore_wait(barrier, len(peers))

    def block(zz, yy):
        return rows.at[pl.ds(first(zz, c, yy), regions)]

    def shared(zz, cc):
        return rows.at[pl.ds(first(zz, cc, 0), group)]

    def push(ref, ssem, rsem, dev):
        go(ref, ref, ssem, rsem, dev)

    def land(ref, ssem, rsem):
        copy(ref, ref, ssem, rsem, at(z, y, c)).wait_recv()

    def around(k, ref):
        for j, yy in ((0, across), (1, right), (2, left)):
            push(ref, gy_s.at[k, j], gy_r.at[k, j], at(z, yy, c))

    def around_landed(k):
        zz = (z + NZ - k) % NZ
        for j, yy in ((1, left), (2, right), (0, across)):
            land(block(zz, yy), gy_s.at[k, j], gy_r.at[k, j])

    def beside(j, yy):
        for i, d in enumerate(BESIDE):
            push(block(z, yy), gv_s.at[i, j], gv_r.at[i, j], at((z + d) % NZ, y, c))

    def to_partner(k):
        push(shared((z + NZ - k) % NZ, c), gc_s.at[k], gc_r.at[k], at(z, y, 1 - c))

    beside(0, y)
    around(0, block(z, y))
    for d in FAR:
        push(block(z, y), gz_s.at[d], gz_r.at[d], at((z + d) % NZ, y, c))
    for n in range(regions):
        for q in range(CHUNKS):
            block_load(n, q).start()

    for one in loads[4:6]:
        one.wait()
    lanes = iota((slots, total), 1)
    rank = iota((slots, total), 0)
    lane_eye = rank == lanes
    for n in range(regions):
        pick = lanes == me * regions + n
        named = jnp.sum(jnp.where(pick, partners[...], 0), axis=1, keepdims=True)
        length = jnp.sum(jnp.where(pick[:1], lengths[...], 0), axis=1, keepdims=True)
        zz, yy, cc = named // (NY * NC * regions), (named // (NC * regions)) % NY, (named // regions) % NC
        named = first(zz, cc, yy) + named % regions
        live = rank < length
        where = jnp.min(
            jnp.where((named == lanes) & live, rank + n * slots, regions * slots),
            axis=0, keepdims=True,
        )
        table[n : n + 1, :] = where
        whom = jnp.sum(jnp.where(lane_eye, named, 0), axis=0, keepdims=True)
        table[regions + n : regions + n + 1, :] = jnp.where(lanes[:1] == slots, length, whom)
    pushed[regions * slots] = jnp.zeros((episodes, sectors), BF16)

    to_lookup = pltpu.make_async_copy(table, lookup, t_sem.at[0])

    def far_landed(d):
        ref = block((z + NZ - d) % NZ, y)
        land(ref, gz_s.at[d], gz_r.at[d])
        around(d, ref)

    for d in FAR[:2]:
        far_landed(d)
    around_landed(0)
    for j, yy in enumerate((left, right, across)):
        beside(j + 1, yy)
    to_partner(0)
    for d in FAR[2:]:
        far_landed(d)
    to_lookup.start()
    for i, d in enumerate(BESIDE):
        for j, yy in enumerate((y, left, right, across)):
            land(block((z + NZ - d) % NZ, yy), gv_s.at[i, j], gv_r.at[i, j])
        to_partner(d)
    for d in FAR:
        around_landed(d)
        to_partner(d)
    to_lookup.wait()
    for one in loads[6:]:
        one.wait()
    for k in (0,) + BESIDE + FAR:
        land(shared((z + NZ - k) % NZ, 1 - c), gc_s.at[k], gc_r.at[k])

    def importer(n, carry):
        slope = -elasticity[...]
        length = lookup[regions + n, slots]
        top = jnp.full((episodes, sectors), -jnp.inf, F32)
        for q in range(CHUNKS):
            block_load(n, q).wait()
            for s in range(q * step, (q + 1) * step):
                landed = tau[n, s : s + 1, :] + jnp.dot(
                    rows[lookup[regions + n, s]], held[n, s], preferred_element_type=F32
                )
                score = jnp.where(s < length, slope * landed, -jnp.inf)
                weights[s] = score
                top = jnp.maximum(top, score)
        summed = jnp.zeros((episodes, sectors), F32)
        for s in range(slots):
            one = jnp.exp(weights[s] - top)
            weights[s] = one
            summed = summed + one
        prices_out[n] = (-(top + jnp.log(summed)) / elasticity[...]).astype(BF16)
        scale = cot[n] / summed
        for s in range(slots):
            one = weights[s] * scale
            tau_part[n, s : s + 1, :] = jnp.sum(one, axis=0, keepdims=True)
            pushed[n * slots + s] = lax.dot_general(
                one.astype(BF16), held[n, s], (((1,), (1,)), ((), ())),
                preferred_element_type=F32,
            ).astype(BF16)
        return carry

    lax.fori_loop(0, regions, importer, 0)

    def fill(dst, k, cc):
        base = first((z + ORDER[k]) % NZ, cc, 0)

        def some(r, carry):
            for i in range(regions):
                at_row = r * regions + i
                value = pushed[lookup[0, base + at_row]].astype(F32)
                for n in range(1, regions):
                    value = value + pushed[lookup[n, base + at_row]].astype(F32)
                dst[k, at_row] = value.astype(BF16)
            return carry

        lax.fori_loop(0, NY, some, 0)

    core_moves = []
    for k in range(NZ):
        fill(outgo, k, 1 - c)
        core_moves.append(
            go(outgo.at[k], from_core.at[k], c_s.at[k], c_r.at[k], at(z, y, 1 - c))
        )
    tau_moves = [
        go(tau_part, x_in.at[here], x_s.at[d], x_r.at[d], {"ep": (here + d) % size})
        for d in range(1, size)
    ]
    x_in[here] = tau_part[...]
    for k in range(NZ):
        fill(own, k, c)

    def chip(k, yy):
        part = pl.ds(yy * regions, regions)
        return own[k, part].astype(F32) + from_core[k, part].astype(F32)

    ways = ((0, across), (1, right), (2, left))
    y_moves, z_moves, v_moves = {}, [], []

    def send_around(k, value):
        for j, yy in ways:
            near[k, j] = value(yy).astype(BF16)
        y_moves[k] = [
            go(near.at[k, j], y_in.at[k, j], y_s.at[k, j], y_r.at[k, j], at(z, yy, c))
            for j, yy in ways
        ]

    def came_around(k):
        value = None
        for j in (1, 2, 0):
            y_moves[k][j].wait_recv()
            term = y_in[k, j].astype(F32)
            value = term if value is None else value + term
        return value

    for k in range(NZ - 1):
        core_moves[k].wait_recv()
        d = ORDER[k]
        if d in BESIDE:
            i = BESIDE.index(d)
            for r in range(NY):
                part = pl.ds(r * regions, regions)
                slab[i, part] = chip(k, r).astype(BF16)
            v_moves.append(
                go(slab.at[i], v_in.at[i], v_s.at[i], v_r.at[i], at((z + d) % NZ, y, c))
            )
        else:
            send_around(k, lambda yy: chip(k, yy))

    def send_far(k):
        mine[k] = (chip(k, y) + came_around(k)).astype(BF16)
        z_moves.append((k, go(
            mine.at[k], z_in.at[k], z_s.at[k], z_r.at[k], at((z + ORDER[k]) % NZ, y, c)
        )))

    last = NZ - 1
    far = [k for k in range(last) if ORDER[k] not in BESIDE]
    for k in far[:2]:
        send_far(k)
    core_moves[last].wait_recv()
    for one in v_moves:
        one.wait_recv()

    def own_chunk(yy):
        part = pl.ds(yy * regions, regions)
        return chip(last, yy) + (v_in[0, part].astype(F32) + v_in[1, part].astype(F32))

    send_around(last, own_chunk)
    for k in far[2:]:
        send_far(k)
    for one in tau_moves:
        one.wait_recv()
    tau_sum[...] = (x_in[0] + x_in[1]) + (x_in[2] + x_in[3])
    final = own_chunk(y) + came_around(last)
    for k, one in z_moves[::-1]:
        one.wait_recv()
        final = final + z_in[k].astype(F32)
    for i in range(regions):
        price_grad[i] = lax.dot_general(
            final[i].astype(BF16), io[i], (((1,), (1,)), ((), ())), preferred_element_type=F32
        )
        column = jnp.sum(final[i] * share[i : i + 1, :], axis=1, keepdims=True)
        wage_grad[i : i + 1, :] = jnp.sum(jnp.where(eye, column, 0.0), axis=0, keepdims=True)
    for one in sends:
        one.wait_send()


def finish_kernel(*refs):
    count = (len(refs) - 2) // 3
    source, result, held = refs[:count], refs[count : 2 * count], refs[2 * count : 3 * count]
    in_sem, out_sem = refs[-2:]
    ins = [pltpu.make_async_copy(source[i], held[i], in_sem.at[i]) for i in range(count)]
    outs = [pltpu.make_async_copy(held[i], result[i], out_sem.at[i]) for i in range(count)]
    for one in ins:
        one.start()
    for one, then in zip(ins, outs):
        one.wait()
        then.start()
    for one in outs:
        one.wait()


def shards(
    log_prices,
    log_wages,
    labor_share,
    io_coeffs,
    pair_blocks,
    log_tau,
    elasticity,
    partners,
    list_lengths,
    price_cotangent,
):
    own, episodes, sectors = log_prices.shape
    slots = pair_blocks.shape[1]
    block = (own, episodes, sectors)
    group = (NY * own, episodes, sectors)
    total = NZ * NY * NC * own
    tau_shape = (own, slots, sectors)
    vm = pltpu.VMEM
    outs = (
        jax.ShapeDtypeStruct(block, BF16),
        jax.ShapeDtypeStruct(block, F32),
        jax.ShapeDtypeStruct((own, episodes), F32),
        jax.ShapeDtypeStruct(tau_shape, F32),
    )
    results = pl.pallas_call(
        fused_kernel,
        out_shape=outs,
        in_specs=[ANY] * 10,
        out_specs=(VMEM,) * 4,
        scratch_shapes=[
            vm(block, BF16), vm((own, episodes), F32), vm((own, sectors), F32),
            vm((own, sectors, sectors), BF16), vm(tau_shape, F32), vm((1, sectors), F32),
            vm((slots, total), I32), vm((1, total), I32), vm(block, F32),
            vm((own, slots, sectors, sectors), BF16), DMA((9,)), DMA((own * CHUNKS,)),
            vm((2 * own, total), I32), pltpu.SMEM((2 * own, total), I32), DMA((1,)),
            vm((total, episodes, sectors), BF16), vm((slots, episodes, sectors), F32),
            vm((own * slots + 1, episodes, sectors), BF16), vm(tau_shape, F32),
            vm((NZ,) + group, BF16), vm((NZ,) + group, BF16), vm((NZ,) + group, BF16),
            vm((NZ, 3) + block, BF16), vm((NZ, 3) + block, BF16), vm((2,) + group, BF16),
            vm((2,) + group, BF16), vm((NZ,) + block, BF16), vm((NZ,) + block, BF16),
            vm((4,) + tau_shape, F32),
            DMA((NZ,)), DMA((NZ,)), DMA((NZ, 3)), DMA((NZ, 3)), DMA((2, 4)), DMA((2, 4)),
            DMA((NZ,)), DMA((NZ,)),
            DMA((NZ,)), DMA((NZ,)), DMA((NZ, 3)), DMA((NZ, 3)), DMA((2,)), DMA((2,)),
            DMA((NZ,)), DMA((NZ,)), DMA((4,)), DMA((4,)),
        ],
        compiler_params=pltpu.CompilerParams(
            collective_id=0, has_side_effects=True, vmem_limit_bytes=60 * 1024 * 1024
        ),
        name="iteration",
    )(
        log_prices, log_wages, labor_share, io_coeffs, pair_blocks, log_tau,
        elasticity.reshape(1, sectors), partners.T, list_lengths.reshape(1, total),
        price_cotangent,
    )
    return pl.pallas_call(
        finish_kernel,
        out_shape=outs,
        in_specs=[ANY] * 4,
        out_specs=(ANY,) * 4,
        scratch_shapes=[vm(one.shape, one.dtype) for one in outs] + [DMA((4,)), DMA((4,))],
        compiler_params=pltpu.CompilerParams(vmem_limit_bytes=60 * 1024 * 1024),
        name="finish",
    )(*results)


def solution(mesh):
    return jax.shard_map(
        shards,
        mesh=mesh,
        in_specs=(
            P("reg", "ep", None),
            P("reg", "ep"),
            P("reg", None),
            P("reg", None, None),
            P("reg", None, None, None),
            P("reg", None, None),
            P(),
            P(),
            P(),
            P("reg", "ep", None),
        ),
        out_specs=(
            P("reg", "ep", None),
            P("reg", "ep", None),
            P("reg", "ep"),
            P("reg", None, None),
        ),
        check_vma=False,
    )
```

```python
import jax
import jax.numpy as jnp
from jax import lax
from jax.experimental import pallas as pl
from jax.experimental.pallas import tpu as pltpu
from jax.sharding import PartitionSpec as P

NZ, NY, NC = 8, 4, 2
FAR = (2, 6, 3, 5, 4)
BESIDE = (1, 7)
ORDER = (4, 5, 3, 1, 7, 6, 2, 0)
CHUNKS = 4
LOG2E, LN2 = 1.4426950408889634, 0.6931471805599453
F32 = jnp.float32
BF16 = jnp.bfloat16
I32 = jnp.int32
MESH = pl.DeviceIdType.MESH
VMEM = pl.BlockSpec(memory_space=pltpu.VMEM)
ANY = pl.BlockSpec(memory_space=pl.ANY)
DMA = pltpu.SemaphoreType.DMA


def at(z, y, c):
    return {"reg": (z * NY + y) * NC + c}


def iota(shape, axis):
    return lax.broadcasted_iota(I32, shape, axis)


def fused_kernel(
    prices_in, wages_in, share_in, io_in, blocks, tau_in, slope_in, partners_in, lengths_in, cot_in,
    prices_out, price_grad, wage_grad, tau_sum,
    prices, wages, share, io, tau, elasticity, partners, lengths, cot, held, in_sem, b_sem,
    table, lookup, t_sem,
    rows, weights, pushed, tau_part,
    outgo, own, from_core, near, y_in, slab, v_in, mine, z_in, x_in,
    gz_s, gz_r, gy_s, gy_r, gv_s, gv_r, gc_s, gc_r,
    c_s, c_r, y_s, y_r, v_s, v_r, z_s, z_r, x_s, x_r,
):
    me = lax.axis_index("reg")
    z, y, c = me // (NY * NC), (me // NC) % NY, me % NC
    here, size = lax.axis_index("ep"), lax.axis_size("ep")
    right, left, across = (y + 1) % NY, (y + NY - 1) % NY, (y + 2) % NY
    regions, slots = blocks.shape[0], blocks.shape[1]
    episodes, sectors = cot.shape[1], cot.shape[2]
    total = rows.shape[0]
    group = NY * regions

    barrier = pltpu.get_barrier_semaphore()
    peers = [at((z + d) % NZ, y, c) for d in range(1, NZ)]
    peers += [at(z, right, c), at(z, left, c), at(z, across, c), at(z, y, 1 - c)]
    peers += [{"ep": (here + d) % size} for d in range(1, size)]
    for peer in peers:
        pl.semaphore_signal(barrier, inc=1, device_id=peer, device_id_type=MESH)

    loads = [
        pltpu.make_async_copy(src, dst, in_sem.at[i])
        for i, (src, dst) in enumerate(
            (
                (io_in, io), (prices_in, prices), (wages_in, wages), (share_in, share),
                (partners_in, partners), (lengths_in, lengths), (slope_in, elasticity),
                (tau_in, tau), (cot_in, cot),
            )
        )
    ]
    for one in loads:
        one.start()
    step = slots // CHUNKS

    def block_load(n, q):
        part = pl.ds(q * step, step)
        return pltpu.make_async_copy(
            blocks.at[n, part], held.at[n, part], b_sem.at[n * CHUNKS + q]
        )

    sends = []

    def copy(src, dst, ssem, rsem, dev):
        return pltpu.make_async_remote_copy(
            src_ref=src, dst_ref=dst, send_sem=ssem, recv_sem=rsem,
            device_id=dev, device_id_type=MESH,
        )

    def go(*args):
        one = copy(*args)
        one.start()
        sends.append(one)
        return one

    def first(zz, cc, yy):
        return ((zz * NC + cc) * NY + yy) * regions

    for one in loads[:4]:
        one.wait()
    eye = iota((episodes, episodes), 0) == iota((episodes, episodes), 1)
    for i in range(regions):
        column = jnp.sum(jnp.where(eye, wages[i : i + 1, :], 0.0), axis=1, keepdims=True)
        unit = column * share[i : i + 1, :] + jnp.dot(
            prices[i], io[i], preferred_element_type=F32
        )
        rows[first(z, c, y) + i] = unit.astype(BF16)
    pl.semaphore_wait(barrier, len(peers))

    def block(zz, yy):
        return rows.at[pl.ds(first(zz, c, yy), regions)]

    def shared(zz, cc):
        return rows.at[pl.ds(first(zz, cc, 0), group)]

    def push(ref, ssem, rsem, dev):
        go(ref, ref, ssem, rsem, dev)

    def land(ref, ssem, rsem):
        copy(ref, ref, ssem, rsem, at(z, y, c)).wait_recv()

    def around(k, ref):
        for j, yy in ((0, across), (1, right), (2, left)):
            push(ref, gy_s.at[k, j], gy_r.at[k, j], at(z, yy, c))

    def around_landed(k):
        zz = (z + NZ - k) % NZ
        for j, yy in ((1, left), (2, right), (0, across)):
            land(block(zz, yy), gy_s.at[k, j], gy_r.at[k, j])

    def beside(j, yy):
        for i, d in enumerate(BESIDE):
            push(block(z, yy), gv_s.at[i, j], gv_r.at[i, j], at((z + d) % NZ, y, c))

    def to_partner(k):
        push(shared((z + NZ - k) % NZ, c), gc_s.at[k], gc_r.at[k], at(z, y, 1 - c))

    beside(0, y)
    around(0, block(z, y))
    for d in FAR:
        push(block(z, y), gz_s.at[d], gz_r.at[d], at((z + d) % NZ, y, c))
    for n in range(regions):
        for q in range(CHUNKS):
            block_load(n, q).start()

    for one in loads[4:6]:
        one.wait()
    lanes = iota((slots, total), 1)
    rank = iota((slots, total), 0)
    lane_eye = rank == lanes
    for n in range(regions):
        pick = lanes == me * regions + n
        named = jnp.sum(jnp.where(pick, partners[...], 0), axis=1, keepdims=True)
        length = jnp.sum(jnp.where(pick[:1], lengths[...], 0), axis=1, keepdims=True)
        zz, yy, cc = named // (NY * NC * regions), (named // (NC * regions)) % NY, (named // regions) % NC
        named = first(zz, cc, yy) + named % regions
        live = rank < length
        where = jnp.min(
            jnp.where((named == lanes) & live, rank + n * slots, regions * slots),
            axis=0, keepdims=True,
        )
        table[n : n + 1, :] = where
        whom = jnp.sum(jnp.where(lane_eye, named, 0), axis=0, keepdims=True)
        table[regions + n : regions + n + 1, :] = jnp.where(lanes[:1] == slots, length, whom)
    pushed[regions * slots] = jnp.zeros((episodes, sectors), BF16)

    to_lookup = pltpu.make_async_copy(table, lookup, t_sem.at[0])

    def far_landed(d):
        ref = block((z + NZ - d) % NZ, y)
        land(ref, gz_s.at[d], gz_r.at[d])
        around(d, ref)

    for d in FAR[:2]:
        far_landed(d)
    around_landed(0)
    for j, yy in enumerate((left, right, across)):
        beside(j + 1, yy)
    to_partner(0)
    for d in FAR[2:]:
        far_landed(d)
    to_lookup.start()
    for i, d in enumerate(BESIDE):
        for j, yy in enumerate((y, left, right, across)):
            land(block((z + NZ - d) % NZ, yy), gv_s.at[i, j], gv_r.at[i, j])
        to_partner(d)
    for d in FAR:
        around_landed(d)
        to_partner(d)
    to_lookup.wait()
    for one in loads[6:]:
        one.wait()
    for k in (0,) + BESIDE + FAR:
        land(shared((z + NZ - k) % NZ, 1 - c), gc_s.at[k], gc_r.at[k])

    def importer(n, carry):
        scale2 = elasticity[...] * LOG2E
        slope = -scale2
        length = lookup[regions + n, slots]
        top = jnp.full((episodes, sectors), -jnp.inf, F32)
        for q in range(CHUNKS):
            block_load(n, q).wait()
            for s in range(q * step, (q + 1) * step):
                landed = tau[n, s : s + 1, :] + jnp.dot(
                    rows[lookup[regions + n, s]], held[n, s], preferred_element_type=F32
                )
                score = jnp.where(s < length, slope * landed, -jnp.inf)
                weights[s] = score
                top = jnp.maximum(top, score)
        summed = jnp.zeros((episodes, sectors), F32)
        for s in range(slots):
            one = jnp.exp2(weights[s] - top)
            weights[s] = one
            summed = summed + one
        prices_out[n] = (-(top * LN2 + jnp.log(summed)) / elasticity[...]).astype(BF16)
        scale = cot[n] / summed
        for s in range(slots):
            one = weights[s] * scale
            tau_part[n, s : s + 1, :] = jnp.sum(one, axis=0, keepdims=True)
            pushed[n * slots + s] = lax.dot_general(
                one.astype(BF16), held[n, s], (((1,), (1,)), ((), ())),
                preferred_element_type=F32,
            ).astype(BF16)
        return carry

    lax.fori_loop(0, regions, importer, 0)

    def fill(dst, k, cc):
        base = first((z + ORDER[k]) % NZ, cc, 0)

        for at_row in range(group):
            terms = [pushed[lookup[n, base + at_row]] for n in range(regions)]
            while len(terms) > 1:
                terms = [sum(terms[j + 1 : j + 2], terms[j]) for j in range(0, len(terms), 2)]
            dst[k, at_row] = terms[0]

    core_moves = []
    for k in range(NZ):
        fill(outgo, k, 1 - c)
        core_moves.append(
            go(outgo.at[k], from_core.at[k], c_s.at[k], c_r.at[k], at(z, y, 1 - c))
        )
    tau_moves = [
        go(tau_part, x_in.at[here], x_s.at[d], x_r.at[d], {"ep": (here + d) % size})
        for d in range(1, size)
    ]
    x_in[here] = tau_part[...]
    def chip(k, yy):
        part = pl.ds(yy * regions, regions)
        return own[k, part].astype(F32) + from_core[k, part].astype(F32)

    ways = ((0, across), (1, right), (2, left))
    y_moves, z_moves, v_moves = {}, [], []

    def send_around(k, value):
        for j, yy in ways:
            near[k, j] = value(yy).astype(BF16)
        y_moves[k] = [
            go(near.at[k, j], y_in.at[k, j], y_s.at[k, j], y_r.at[k, j], at(z, yy, c))
            for j, yy in ways
        ]

    def came_around(k):
        value = None
        for j in (1, 2, 0):
            y_moves[k][j].wait_recv()
            term = y_in[k, j].astype(F32)
            value = term if value is None else value + term
        return value

    for k in range(NZ - 1):
        fill(own, k, c)
        core_moves[k].wait_recv()
        d = ORDER[k]
        if d in BESIDE:
            i = BESIDE.index(d)
            for r in range(NY):
                part = pl.ds(r * regions, regions)
                slab[i, part] = chip(k, r).astype(BF16)
            v_moves.append(
                go(slab.at[i], v_in.at[i], v_s.at[i], v_r.at[i], at((z + d) % NZ, y, c))
            )
        else:
            send_around(k, lambda yy: chip(k, yy))

    def send_far(k):
        mine[k] = (chip(k, y) + came_around(k)).astype(BF16)
        z_moves.append((k, go(
            mine.at[k], z_in.at[k], z_s.at[k], z_r.at[k], at((z + ORDER[k]) % NZ, y, c)
        )))

    last = NZ - 1
    far = [k for k in range(last) if ORDER[k] not in BESIDE]
    for k in far[:2]:
        send_far(k)
    fill(own, last, c)
    core_moves[last].wait_recv()
    for one in v_moves:
        one.wait_recv()

    def own_chunk(yy):
        part = pl.ds(yy * regions, regions)
        return chip(last, yy) + (v_in[0, part].astype(F32) + v_in[1, part].astype(F32))

    send_around(last, own_chunk)
    for k in far[2:]:
        send_far(k)
    for one in tau_moves:
        one.wait_recv()
    tau_sum[...] = (x_in[0] + x_in[1]) + (x_in[2] + x_in[3])
    final = own_chunk(y) + came_around(last)
    for k, one in z_moves[::-1]:
        one.wait_recv()
        final = final + z_in[k].astype(F32)
    for i in range(regions):
        price_grad[i] = lax.dot_general(
            final[i].astype(BF16), io[i], (((1,), (1,)), ((), ())), preferred_element_type=F32
        )
        column = jnp.sum(final[i] * share[i : i + 1, :], axis=1, keepdims=True)
        wage_grad[i : i + 1, :] = jnp.sum(jnp.where(eye, column, 0.0), axis=0, keepdims=True)
    for one in sends:
        one.wait_send()


def finish_kernel(*refs):
    count = (len(refs) - 2) // 3
    source, result, held = refs[:count], refs[count : 2 * count], refs[2 * count : 3 * count]
    in_sem, out_sem = refs[-2:]
    ins = [pltpu.make_async_copy(source[i], held[i], in_sem.at[i]) for i in range(count)]
    outs = [pltpu.make_async_copy(held[i], result[i], out_sem.at[i]) for i in range(count)]
    for one in ins:
        one.start()
    for one, then in zip(ins, outs):
        one.wait()
        then.start()
    for one in outs:
        one.wait()


def shards(
    log_prices,
    log_wages,
    labor_share,
    io_coeffs,
    pair_blocks,
    log_tau,
    elasticity,
    partners,
    list_lengths,
    price_cotangent,
):
    own, episodes, sectors = log_prices.shape
    slots = pair_blocks.shape[1]
    block = (own, episodes, sectors)
    group = (NY * own, episodes, sectors)
    total = NZ * NY * NC * own
    tau_shape = (own, slots, sectors)
    vm = pltpu.VMEM
    outs = (
        jax.ShapeDtypeStruct(block, BF16),
        jax.ShapeDtypeStruct(block, F32),
        jax.ShapeDtypeStruct((own, episodes), F32),
        jax.ShapeDtypeStruct(tau_shape, F32),
    )
    results = pl.pallas_call(
        fused_kernel,
        out_shape=outs,
        in_specs=[ANY] * 10,
        out_specs=(VMEM,) * 4,
        scratch_shapes=[
            vm(block, BF16), vm((own, episodes), F32), vm((own, sectors), F32),
            vm((own, sectors, sectors), BF16), vm(tau_shape, F32), vm((1, sectors), F32),
            vm((slots, total), I32), vm((1, total), I32), vm(block, F32),
            vm((own, slots, sectors, sectors), BF16), DMA((9,)), DMA((own * CHUNKS,)),
            vm((2 * own, total), I32), pltpu.SMEM((2 * own, total), I32), DMA((1,)),
            vm((total, episodes, sectors), BF16), vm((slots, episodes, sectors), F32),
            vm((own * slots + 1, episodes, sectors), BF16), vm(tau_shape, F32),
            vm((NZ,) + group, BF16), vm((NZ,) + group, BF16), vm((NZ,) + group, BF16),
            vm((NZ, 3) + block, BF16), vm((NZ, 3) + block, BF16), vm((2,) + group, BF16),
            vm((2,) + group, BF16), vm((NZ,) + block, BF16), vm((NZ,) + block, BF16),
            vm((4,) + tau_shape, F32),
            DMA((NZ,)), DMA((NZ,)), DMA((NZ, 3)), DMA((NZ, 3)), DMA((2, 4)), DMA((2, 4)),
            DMA((NZ,)), DMA((NZ,)),
            DMA((NZ,)), DMA((NZ,)), DMA((NZ, 3)), DMA((NZ, 3)), DMA((2,)), DMA((2,)),
            DMA((NZ,)), DMA((NZ,)), DMA((4,)), DMA((4,)),
        ],
        compiler_params=pltpu.CompilerParams(
            collective_id=0, has_side_effects=True, vmem_limit_bytes=60 * 1024 * 1024
        ),
        name="iteration",
    )(
        log_prices, log_wages, labor_share, io_coeffs, pair_blocks, log_tau,
        elasticity.reshape(1, sectors), partners.T, list_lengths.reshape(1, total),
        price_cotangent,
    )
    return pl.pallas_call(
        finish_kernel,
        out_shape=outs,
        in_specs=[ANY] * 4,
        out_specs=(ANY,) * 4,
        scratch_shapes=[vm(one.shape, one.dtype) for one in outs] + [DMA((4,)), DMA((4,))],
        compiler_params=pltpu.CompilerParams(vmem_limit_bytes=60 * 1024 * 1024),
        name="finish",
    )(*results)


def solution(mesh):
    return jax.shard_map(
        shards,
        mesh=mesh,
        in_specs=(
            P("reg", "ep", None),
            P("reg", "ep"),
            P("reg", None),
            P("reg", None, None),
            P("reg", None, None, None),
            P("reg", None, None),
            P(),
            P(),
            P(),
            P("reg", "ep", None),
        ),
        out_specs=(
            P("reg", "ep", None),
            P("reg", "ep", None),
            P("reg", "ep"),
            P("reg", None, None),
        ),
        check_vma=False,
    )
```

```python
import jax
import jax.numpy as jnp
from jax import lax
from jax.experimental import pallas as pl
from jax.experimental.pallas import tpu as pltpu
from jax.sharding import PartitionSpec as P

NZ, NY, NC = 8, 4, 2
FAR = (2, 6, 3, 5, 4)
BESIDE = (1, 7)
ORDER = (4, 5, 3, 1, 7, 6, 2, 0)
CHUNKS = 4
LEAD = 4
LOG2E, LN2 = 1.4426950408889634, 0.6931471805599453
F32 = jnp.float32
BF16 = jnp.bfloat16
I32 = jnp.int32
MESH = pl.DeviceIdType.MESH
VMEM = pl.BlockSpec(memory_space=pltpu.VMEM)
ANY = pl.BlockSpec(memory_space=pl.ANY)
DMA = pltpu.SemaphoreType.DMA


def at(z, y, c):
    return {"reg": (z * NY + y) * NC + c}


def iota(shape, axis):
    return lax.broadcasted_iota(I32, shape, axis)


def fused_kernel(
    prices_in, wages_in, share_in, io_in, blocks, tau_in, slope_in, partners_in, lengths_in, cot_in,
    prices_out, price_grad, wage_grad, tau_sum,
    prices, wages, share, io, tau, elasticity, partners, lengths, cot, held, in_sem, b_sem,
    table, lookup, t_sem,
    rows, weights, pushed, tau_part,
    outgo, own, from_core, near, y_in, slab, v_in, mine, z_in, x_in,
    gz_s, gz_r, gy_s, gy_r, gv_s, gv_r, gc_s, gc_r,
    c_s, c_r, y_s, y_r, v_s, v_r, z_s, z_r, x_s, x_r,
):
    me = lax.axis_index("reg")
    z, y, c = me // (NY * NC), (me // NC) % NY, me % NC
    here, size = lax.axis_index("ep"), lax.axis_size("ep")
    right, left, across = (y + 1) % NY, (y + NY - 1) % NY, (y + 2) % NY
    regions, slots = blocks.shape[0], blocks.shape[1]
    episodes, sectors = cot.shape[1], cot.shape[2]
    total = rows.shape[0]
    group = NY * regions

    barrier = pltpu.get_barrier_semaphore()
    peers = [at((z + d) % NZ, y, c) for d in range(1, NZ)]
    peers += [at(z, right, c), at(z, left, c), at(z, across, c), at(z, y, 1 - c)]
    peers += [{"ep": (here + d) % size} for d in range(1, size)]
    for peer in peers:
        pl.semaphore_signal(barrier, inc=1, device_id=peer, device_id_type=MESH)

    loads = [
        pltpu.make_async_copy(src, dst, in_sem.at[i])
        for i, (src, dst) in enumerate(
            (
                (io_in, io), (prices_in, prices), (wages_in, wages), (share_in, share),
                (partners_in, partners), (lengths_in, lengths), (slope_in, elasticity),
                (tau_in, tau), (cot_in, cot),
            )
        )
    ]
    for one in loads:
        one.start()
    step = slots // CHUNKS

    def block_load(n, q):
        part = pl.ds(q * step, step)
        return pltpu.make_async_copy(
            blocks.at[n, part], held.at[n, part], b_sem.at[n * CHUNKS + q]
        )

    sends = []

    def copy(src, dst, ssem, rsem, dev):
        return pltpu.make_async_remote_copy(
            src_ref=src, dst_ref=dst, send_sem=ssem, recv_sem=rsem,
            device_id=dev, device_id_type=MESH,
        )

    def go(*args):
        one = copy(*args)
        one.start()
        sends.append(one)
        return one

    def first(zz, cc, yy):
        return ((zz * NC + cc) * NY + yy) * regions

    for one in loads[:4]:
        one.wait()
    eye = iota((episodes, episodes), 0) == iota((episodes, episodes), 1)
    for i in range(regions):
        column = jnp.sum(jnp.where(eye, wages[i : i + 1, :], 0.0), axis=1, keepdims=True)
        unit = column * share[i : i + 1, :] + jnp.dot(
            prices[i], io[i], preferred_element_type=F32
        )
        rows[first(z, c, y) + i] = unit.astype(BF16)
    pl.semaphore_wait(barrier, len(peers))

    def block(zz, yy):
        return rows.at[pl.ds(first(zz, c, yy), regions)]

    def shared(zz, cc):
        return rows.at[pl.ds(first(zz, cc, 0), group)]

    def push(ref, ssem, rsem, dev):
        go(ref, ref, ssem, rsem, dev)

    def land(ref, ssem, rsem):
        copy(ref, ref, ssem, rsem, at(z, y, c)).wait_recv()

    def around(k, ref):
        for j, yy in ((0, across), (1, right), (2, left)):
            push(ref, gy_s.at[k, j], gy_r.at[k, j], at(z, yy, c))

    def around_landed(k):
        zz = (z + NZ - k) % NZ
        for j, yy in ((1, left), (2, right), (0, across)):
            land(block(zz, yy), gy_s.at[k, j], gy_r.at[k, j])

    def beside(j, yy):
        for i, d in enumerate(BESIDE):
            push(block(z, yy), gv_s.at[i, j], gv_r.at[i, j], at((z + d) % NZ, y, c))

    def to_partner(k):
        push(shared((z + NZ - k) % NZ, c), gc_s.at[k], gc_r.at[k], at(z, y, 1 - c))

    beside(0, y)
    around(0, block(z, y))
    for d in FAR:
        push(block(z, y), gz_s.at[d], gz_r.at[d], at((z + d) % NZ, y, c))
    for n in range(regions):
        for q in range(CHUNKS):
            block_load(n, q).start()

    for one in loads[4:6]:
        one.wait()
    lanes = iota((slots, total), 1)
    rank = iota((slots, total), 0)
    lane_eye = rank == lanes
    for n in range(regions):
        pick = lanes == me * regions + n
        named = jnp.sum(jnp.where(pick, partners[...], 0), axis=1, keepdims=True)
        length = jnp.sum(jnp.where(pick[:1], lengths[...], 0), axis=1, keepdims=True)
        zz, yy, cc = named // (NY * NC * regions), (named // (NC * regions)) % NY, (named // regions) % NC
        named = first(zz, cc, yy) + named % regions
        live = rank < length
        where = jnp.min(
            jnp.where((named == lanes) & live, rank + n * slots, regions * slots),
            axis=0, keepdims=True,
        )
        table[n : n + 1, :] = where
        whom = jnp.sum(jnp.where(lane_eye, named, 0), axis=0, keepdims=True)
        table[regions + n : regions + n + 1, :] = jnp.where(lanes[:1] == slots, length, whom)
    pushed[regions * slots] = jnp.zeros((episodes, sectors), BF16)

    to_lookup = pltpu.make_async_copy(table, lookup, t_sem.at[0])

    def far_landed(d):
        ref = block((z + NZ - d) % NZ, y)
        land(ref, gz_s.at[d], gz_r.at[d])
        around(d, ref)

    for d in FAR[:2]:
        far_landed(d)
    around_landed(0)
    for j, yy in enumerate((left, right, across)):
        beside(j + 1, yy)
    to_partner(0)
    for d in FAR[2:]:
        far_landed(d)
    to_lookup.start()
    for i, d in enumerate(BESIDE):
        for j, yy in enumerate((y, left, right, across)):
            land(block((z + NZ - d) % NZ, yy), gv_s.at[i, j], gv_r.at[i, j])
        to_partner(d)
    for d in FAR:
        around_landed(d)
        to_partner(d)
    to_lookup.wait()
    for one in loads[6:]:
        one.wait()
    for k in (0,) + BESIDE + FAR:
        land(shared((z + NZ - k) % NZ, 1 - c), gc_s.at[k], gc_r.at[k])

    def importer(n, carry):
        scale2 = elasticity[...] * LOG2E
        slope = -scale2
        length = lookup[regions + n, slots]
        top = jnp.full((episodes, sectors), -jnp.inf, F32)
        for q in range(CHUNKS):
            block_load(n, q).wait()
            for s in range(q * step, (q + 1) * step):
                landed = tau[n, s : s + 1, :] + jnp.dot(
                    rows[lookup[regions + n, s]], held[n, s], preferred_element_type=F32
                )
                score = jnp.where(s < length, slope * landed, -jnp.inf)
                weights[s] = score
                top = jnp.maximum(top, score)
        summed = jnp.zeros((episodes, sectors), F32)
        for s in range(slots):
            one = jnp.exp2(weights[s] - top)
            weights[s] = one
            summed = summed + one
        prices_out[n] = (-(top * LN2 + jnp.log(summed)) / elasticity[...]).astype(BF16)
        scale = cot[n] / summed
        for s in range(slots):
            one = weights[s] * scale
            tau_part[n, s : s + 1, :] = jnp.sum(one, axis=0, keepdims=True)
            pushed[n * slots + s] = lax.dot_general(
                one.astype(BF16), held[n, s], (((1,), (1,)), ((), ())),
                preferred_element_type=F32,
            ).astype(BF16)
        return carry

    lax.fori_loop(0, regions, importer, 0)

    def fill(dst, k, cc):
        base = first((z + ORDER[k]) % NZ, cc, 0)

        for at_row in range(group):
            terms = [pushed[lookup[n, base + at_row]] for n in range(regions)]
            while len(terms) > 1:
                terms = [sum(terms[j + 1 : j + 2], terms[j]) for j in range(0, len(terms), 2)]
            dst[k, at_row] = terms[0]

    core_moves = []

    def cross(k):
        fill(outgo, k, 1 - c)
        core_moves.append(
            go(outgo.at[k], from_core.at[k], c_s.at[k], c_r.at[k], at(z, y, 1 - c))
        )

    for k in range(LEAD):
        cross(k)
    tau_moves = [
        go(tau_part, x_in.at[here], x_s.at[d], x_r.at[d], {"ep": (here + d) % size})
        for d in range(1, size)
    ]
    x_in[here] = tau_part[...]
    def chip(k, yy):
        part = pl.ds(yy * regions, regions)
        return own[k, part].astype(F32) + from_core[k, part].astype(F32)

    ways = ((0, across), (1, right), (2, left))
    y_moves, z_moves, v_moves = {}, [], []

    def send_around(k, value):
        for j, yy in ways:
            near[k, j] = value(yy).astype(BF16)
        y_moves[k] = [
            go(near.at[k, j], y_in.at[k, j], y_s.at[k, j], y_r.at[k, j], at(z, yy, c))
            for j, yy in ways
        ]

    def came_around(k):
        value = None
        for j in (1, 2, 0):
            y_moves[k][j].wait_recv()
            term = y_in[k, j].astype(F32)
            value = term if value is None else value + term
        return value

    for k in range(NZ - 1):
        if k + LEAD < NZ:
            cross(k + LEAD)
        fill(own, k, c)
        core_moves[k].wait_recv()
        d = ORDER[k]
        if d in BESIDE:
            i = BESIDE.index(d)
            for r in range(NY):
                part = pl.ds(r * regions, regions)
                slab[i, part] = chip(k, r).astype(BF16)
            v_moves.append(
                go(slab.at[i], v_in.at[i], v_s.at[i], v_r.at[i], at((z + d) % NZ, y, c))
            )
        else:
            send_around(k, lambda yy: chip(k, yy))

    def send_far(k):
        mine[k] = (chip(k, y) + came_around(k)).astype(BF16)
        z_moves.append((k, go(
            mine.at[k], z_in.at[k], z_s.at[k], z_r.at[k], at((z + ORDER[k]) % NZ, y, c)
        )))

    last = NZ - 1
    far = [k for k in range(last) if ORDER[k] not in BESIDE]
    for k in far[:2]:
        send_far(k)
    fill(own, last, c)
    core_moves[last].wait_recv()
    for one in v_moves:
        one.wait_recv()

    def own_chunk(yy):
        part = pl.ds(yy * regions, regions)
        return chip(last, yy) + (v_in[0, part].astype(F32) + v_in[1, part].astype(F32))

    send_around(last, own_chunk)
    for k in far[2:]:
        send_far(k)
    for one in tau_moves:
        one.wait_recv()
    tau_sum[...] = (x_in[0] + x_in[1]) + (x_in[2] + x_in[3])
    final = own_chunk(y) + came_around(last)
    for k, one in z_moves[::-1]:
        one.wait_recv()
        final = final + z_in[k].astype(F32)
    for i in range(regions):
        price_grad[i] = lax.dot_general(
            final[i].astype(BF16), io[i], (((1,), (1,)), ((), ())), preferred_element_type=F32
        )
        column = jnp.sum(final[i] * share[i : i + 1, :], axis=1, keepdims=True)
        wage_grad[i : i + 1, :] = jnp.sum(jnp.where(eye, column, 0.0), axis=0, keepdims=True)
    for one in sends:
        one.wait_send()


def finish_kernel(*refs):
    count = (len(refs) - 2) // 3
    source, result, held = refs[:count], refs[count : 2 * count], refs[2 * count : 3 * count]
    in_sem, out_sem = refs[-2:]
    ins = [pltpu.make_async_copy(source[i], held[i], in_sem.at[i]) for i in range(count)]
    outs = [pltpu.make_async_copy(held[i], result[i], out_sem.at[i]) for i in range(count)]
    for one in ins:
        one.start()
    for one, then in zip(ins, outs):
        one.wait()
        then.start()
    for one in outs:
        one.wait()


def shards(
    log_prices,
    log_wages,
    labor_share,
    io_coeffs,
    pair_blocks,
    log_tau,
    elasticity,
    partners,
    list_lengths,
    price_cotangent,
):
    own, episodes, sectors = log_prices.shape
    slots = pair_blocks.shape[1]
    block = (own, episodes, sectors)
    group = (NY * own, episodes, sectors)
    total = NZ * NY * NC * own
    tau_shape = (own, slots, sectors)
    vm = pltpu.VMEM
    outs = (
        jax.ShapeDtypeStruct(block, BF16),
        jax.ShapeDtypeStruct(block, F32),
        jax.ShapeDtypeStruct((own, episodes), F32),
        jax.ShapeDtypeStruct(tau_shape, F32),
    )
    results = pl.pallas_call(
        fused_kernel,
        out_shape=outs,
        in_specs=[ANY] * 10,
        out_specs=(VMEM,) * 4,
        scratch_shapes=[
            vm(block, BF16), vm((own, episodes), F32), vm((own, sectors), F32),
            vm((own, sectors, sectors), BF16), vm(tau_shape, F32), vm((1, sectors), F32),
            vm((slots, total), I32), vm((1, total), I32), vm(block, F32),
            vm((own, slots, sectors, sectors), BF16), DMA((9,)), DMA((own * CHUNKS,)),
            vm((2 * own, total), I32), pltpu.SMEM((2 * own, total), I32), DMA((1,)),
            vm((total, episodes, sectors), BF16), vm((slots, episodes, sectors), F32),
            vm((own * slots + 1, episodes, sectors), BF16), vm(tau_shape, F32),
            vm((NZ,) + group, BF16), vm((NZ,) + group, BF16), vm((NZ,) + group, BF16),
            vm((NZ, 3) + block, BF16), vm((NZ, 3) + block, BF16), vm((2,) + group, BF16),
            vm((2,) + group, BF16), vm((NZ,) + block, BF16), vm((NZ,) + block, BF16),
            vm((4,) + tau_shape, F32),
            DMA((NZ,)), DMA((NZ,)), DMA((NZ, 3)), DMA((NZ, 3)), DMA((2, 4)), DMA((2, 4)),
            DMA((NZ,)), DMA((NZ,)),
            DMA((NZ,)), DMA((NZ,)), DMA((NZ, 3)), DMA((NZ, 3)), DMA((2,)), DMA((2,)),
            DMA((NZ,)), DMA((NZ,)), DMA((4,)), DMA((4,)),
        ],
        compiler_params=pltpu.CompilerParams(
            collective_id=0, has_side_effects=True, vmem_limit_bytes=60 * 1024 * 1024
        ),
        name="iteration",
    )(
        log_prices, log_wages, labor_share, io_coeffs, pair_blocks, log_tau,
        elasticity.reshape(1, sectors), partners.T, list_lengths.reshape(1, total),
        price_cotangent,
    )
    return pl.pallas_call(
        finish_kernel,
        out_shape=outs,
        in_specs=[ANY] * 4,
        out_specs=(ANY,) * 4,
        scratch_shapes=[vm(one.shape, one.dtype) for one in outs] + [DMA((4,)), DMA((4,))],
        compiler_params=pltpu.CompilerParams(vmem_limit_bytes=60 * 1024 * 1024),
        name="finish",
    )(*results)


def solution(mesh):
    return jax.shard_map(
        shards,
        mesh=mesh,
        in_specs=(
            P("reg", "ep", None),
            P("reg", "ep"),
            P("reg", None),
            P("reg", None, None),
            P("reg", None, None, None),
            P("reg", None, None),
            P(),
            P(),
            P(),
            P("reg", "ep", None),
        ),
        out_specs=(
            P("reg", "ep", None),
            P("reg", "ep", None),
            P("reg", "ep"),
            P("reg", None, None),
        ),
        check_vma=False,
    )
```
